128 devices in a mesh: ctx: 8 (over x, core), wide: 16 (over z, y).
Axes of the slice: x: 4, y: 4, z: 4, core: 2. Of those that a mesh axis runs over, the one named last changes fastest.
Arguments:
- tokens: bfloat16 [16384, 2688], P(('ctx', 'wide')), may hold values from -10 to 10
- mamba_gain: float32 [2688], replicated, may hold values from 0.25 to 1.75
- w_z: bfloat16 [2688, 4096], P(None, 'wide'), may hold values from -0.125 to 0.125
- w_x: bfloat16 [2688, 4096], P(None, 'wide'), may hold values from -0.125 to 0.125
- w_bc: bfloat16 [2688, 2048], P(None, 'wide'), may hold values from -0.125 to 0.125
- w_dt: bfloat16 [2688, 64], replicated, may hold values from -1 to 1
- dt_bias: float32 [64], P('wide'), may hold values from -2 to 0
- a_log: float32 [64], P('wide')
- conv_x: float32 [4, 4096], P(None, 'wide'), may hold values from -3 to 3
- conv_bc: float32 [4, 2048], replicated, may hold values from -3 to 3
- skip: float32 [64], P('wide'), may hold values from 0.5 to 1.5
- norm_gain: float32 [4096], P('wide'), may hold values from 0.25 to 1.75
- w_out: bfloat16 [4096, 2688], P('wide'), may hold values from -0.09375 to 0.09375
- moe_gain: float32 [2688], replicated, may hold values from 0.25 to 1.75
- expert_ids: int32 [16384, 6], P(('ctx', 'wide')), may hold values from 0 to 127, all different within a row; in each aligned block of 128 rows (0 to 127, 128 to 255, ...) at most 7 rows name the same one
- router_weights: float32 [16384, 6], P(('ctx', 'wide')), may hold values from 0.05 to 0.5
- w_up: bfloat16 [128, 2688, 1856], P(('ctx', 'wide')), may hold values from -0.125 to 0.125
- w_down: bfloat16 [128, 1856, 2688], P(('ctx', 'wide')), may hold values from -0.125 to 0.125
Outputs:
- mixed: bfloat16 [16384, 2688], P(('ctx', 'wide'))
The draws below stay inside these ranges and needn't reach their ends.
Inputs may be any that keep to these rules, and one draw needn't show every extreme that they name: `expert_ids`: within the rows of one device (128 tokens), no expert is named more than 7 times, and a row names 6 different experts.
All inputs are finite; a program needn't handle non-finite values.
Results may differ from the reference program's by a relative error of at most 0.015.
Values may be sent and summed in bfloat16 or wider, within the bound.
A program may use at most 128 MiB of HBM per device.

```python
import math
import jax
import jax.numpy as jnp
import numpy as np
from jax import lax

D = 2688
HEADS = 64
HEAD_DIM = 64
STATE = 128
GROUPS = 8
KERNEL = 4
FFE = 1856
TOP = 6
BLOCK = 128
TOK_DEV = 128
INNER = 4096
SPAN = 2048
LENGTH = 16384
EXPERTS = 128
CAP = 7
N_CTX = 8
N_WIDE = 16


def shared_direction(key):
    return jax.random.normal(jax.random.fold_in(key, 501), (D,), jnp.float32)


def draw_tokens(key, part):
    direction = shared_direction(key)
    key_noise, key_level = jax.random.split(jax.random.fold_in(key, 23), 2)
    regions = LENGTH // (SPAN // 2)
    levels = jax.random.uniform(key_level, (regions,), jnp.float32, 0.0, 1.5)
    per_row = jnp.repeat(levels, SPAN // 2)
    noise = jax.random.normal(key_noise, (LENGTH, D), jnp.float32)
    values = noise + per_row[:, None] * direction[None, :]
    return jnp.clip(values, -10.0, 10.0).astype(jnp.bfloat16)


def draw_w_dt(key, part):
    direction = shared_direction(key)
    key_noise, key_strength = jax.random.split(jax.random.fold_in(key, 37), 2)
    noise = jax.random.normal(key_noise, (D, HEADS), jnp.float32) / jnp.sqrt(jnp.float32(D))
    strength = jax.random.uniform(key_strength, (HEADS,), jnp.float32, 2.0, 4.0)
    values = noise + direction[:, None] * strength[None, :] / D
    return jnp.clip(values, -1.0, 1.0).astype(jnp.bfloat16)


def draw_a_log(key, part):
    key_slow, key_fast, key_order = jax.random.split(jax.random.fold_in(key, 11), 3)
    slow_rates = jnp.log(jax.random.uniform(key_slow, (HEADS,), jnp.float32, 0.7, 1.5) / LENGTH)
    fast_rates = jax.random.uniform(key_fast, (HEADS,), jnp.float32, jnp.log(0.05), jnp.log(0.2))
    rank_order = jax.random.permutation(key_order, HEADS)
    keep_state = rank_order >= HEADS // 2
    return jnp.where(keep_state, slow_rates, fast_rates)


def block_levels(stream_key, extent, shards, smallest, high):
    factor_of = 1.0
    for position, shards_of in shards:
        steps = jax.random.uniform(jax.random.fold_in(jax.random.fold_in(stream_key, 6), position), (shards_of,), jnp.float32, smallest / len(shards), high / len(shards))
        factor_of = factor_of * jnp.repeat(jnp.exp(steps), extent[position] // shards_of).reshape((-1,) + (1,) * (len(extent) - 1 - position))
    return factor_of


def deal_out(key, own, number, rows, count, top, most, skew):
    order = jax.random.permutation(key, count)
    crowded, ordinary = load_shares(count, rows * top, most, skew, True), load_shares(count, rows * top, most, skew, False)
    places = jnp.arange(count)

    def named(sizes, rotation):
        used = int((sizes > 0).sum())
        fixed = max(1, used // 4)
        passed = fixed + (places - fixed + rotation * (used - fixed)) % max(1, count - fixed)
        return jnp.zeros((count,), jnp.int32).at[order[jnp.where(places < fixed, places, passed)]].set(jnp.asarray(sizes, jnp.int32))

    sizes = jnp.where(number % 4 == 0, named(crowded, number // 4), named(ordinary, number - number // 4 - 1))
    mixed = jax.random.permutation(jax.random.fold_in(own, 3), count)
    giver, sink = mixed[0:count // 2 * 2:2], mixed[1:count // 2 * 2:2]
    slack = jnp.minimum(sizes[giver] - 1, most - sizes[sink]) // 2
    slack = jnp.where((giver == order[0]) | (sink == order[0]) | (sizes[sink] == 0), 0, jnp.maximum(slack, 0))
    passed = jax.random.randint(jax.random.fold_in(own, 4), (count // 2,), 0, 1 << 20) % (slack + 1)
    sizes = sizes.at[giver].add(-passed).at[sink].add(passed)
    labels = jnp.searchsorted(jnp.cumsum(sizes), jnp.arange(rows * top), side="right").astype(jnp.int32)
    listing = labels.reshape(top, rows).T
    listing = listing[jax.random.permutation(jax.random.fold_in(own, 1), rows)]
    rotation = jax.random.randint(jax.random.fold_in(own, 2), (rows, 1), 0, top)
    return jnp.take_along_axis(listing, (jnp.arange(top)[None, :] + rotation) % top, axis=1)


def load_shares(count, total, limit, lean, full):
    loads = [(1 << 20) // math.isqrt(grade ** lean) + 1 for grade in range(1, count + 1)]
    largest = limit if full else min(limit, max(-(-total // count), total * loads[0] // sum(loads)))
    least = 1 if total - largest >= count - 1 else 0
    counts, surplus = [largest] + [least] * (count - 1), total - largest - least * (count - 1)
    while surplus > 0:
        candidates = [i for i in range(1, count) if counts[i] < largest] or [i for i in range(1, count) if counts[i] < limit]
        pool, remaining = sum([loads[i] for i in candidates]), surplus
        for i in candidates:
            more = min(limit - counts[i], max(1, remaining * loads[i] // pool), surplus)
            counts[i] = counts[i] + more
            surplus = surplus - more
    return np.array(counts)


def gaussian(key, extent, width, limit, cuts=(), kind=jnp.bfloat16):
    result = width * jax.random.normal(key, extent, jnp.float32)
    if cuts:
        result = result * block_levels(key, extent, cuts, -0.22, 0.18)
    return jnp.clip(result, -limit, limit).astype(kind)


def setup_inputs(seed: int = 0) -> dict:
    key_list = jax.random.split(jax.random.key(seed), 19)
    tokens = draw_tokens(jax.random.fold_in(key_list[18], 71), 0)
    mamba_gain = jnp.clip(1.0 + 0.15 * jax.random.normal(key_list[1], (D,), jnp.float32), 0.25, 1.75)
    w_z = gaussian(key_list[2], (D, INNER), D ** -0.5, 0.125, ((1, 16),))
    w_x = gaussian(key_list[3], (D, INNER), D ** -0.5, 0.125, ((1, 16),))
    w_bc = gaussian(key_list[4], (D, 2 * GROUPS * STATE), D ** -0.5, 0.125, ((1, 16),))
    w_dt = draw_w_dt(jax.random.fold_in(key_list[18], 71), 0)
    dt_bias = jnp.clip(-2.0 + 2.0 * jax.random.uniform(key_list[6], (HEADS,), jnp.float32) ** block_levels(key_list[6], (HEADS,), ((0, 16),), -0.2, 0.2), -2.0, 0.0)
    a_log = draw_a_log(jax.random.fold_in(key_list[18], 71), 0)
    conv_x = gaussian(key_list[8], (KERNEL, INNER), 0.5, 3.0, ((1, 16),), jnp.float32)
    conv_bc = gaussian(key_list[9], (KERNEL, 2 * GROUPS * STATE), 0.5, 3.0, (), jnp.float32)
    skip = jnp.clip(0.5 + 1.0 * jax.random.uniform(key_list[10], (HEADS,), jnp.float32) ** block_levels(key_list[10], (HEADS,), ((0, 16),), -0.2, 0.2), 0.5, 1.5)
    norm_gain = jnp.clip(1.0 + 0.15 * jax.random.normal(key_list[11], (INNER,), jnp.float32), 0.25, 1.75)
    w_out = gaussian(key_list[12], (INNER, D), INNER ** -0.5, 0.09375, ((0, 16),))
    moe_gain = jnp.clip(1.0 + 0.15 * jax.random.normal(key_list[13], (D,), jnp.float32), 0.25, 1.75)
    expert_ids_keys = jax.random.split(jax.random.fold_in(key_list[14], 1), LENGTH // TOK_DEV)
    expert_ids_turns = jax.random.permutation(jax.random.fold_in(key_list[14], 3), LENGTH // TOK_DEV)
    expert_ids = jax.vmap(lambda own, number: deal_out(jax.random.fold_in(key_list[14], 2), own, number, TOK_DEV, EXPERTS, TOP, CAP, 2))(expert_ids_keys, expert_ids_turns).reshape((LENGTH, TOP))
    router_weights = jnp.clip(jnp.exp(math.log(0.5) - 2.3025851 * jax.random.uniform(key_list[15], (LENGTH, TOP), jnp.float32) ** block_levels(key_list[15], (LENGTH, TOP), ((0, 128),), -0.2, 0.2)), 0.05, 0.5)
    w_up = gaussian(key_list[16], (EXPERTS, D, FFE), D ** -0.5, 0.125, ((0, 128),))
    w_down = gaussian(key_list[17], (EXPERTS, FFE, D), FFE ** -0.5, 0.125, ((0, 128),))
    return dict(tokens=tokens, mamba_gain=mamba_gain, w_z=w_z, w_x=w_x, w_bc=w_bc, w_dt=w_dt, dt_bias=dt_bias, a_log=a_log, conv_x=conv_x, conv_bc=conv_bc, skip=skip, norm_gain=norm_gain, w_out=w_out, moe_gain=moe_gain, expert_ids=expert_ids, router_weights=router_weights, w_up=w_up, w_down=w_down)


EPSILON = 1e-05
PRECISE = lax.Precision.HIGHEST

def rms_scale(values, gain_vec):
    mean_sq = lax.optimization_barrier(jnp.mean(values * values, axis=-1, keepdims=True))
    return values * lax.rsqrt(mean_sq + EPSILON) * gain_vec

def causal_conv(pre_conv, taps):
    length = pre_conv.shape[0]
    padded = jnp.concatenate([jnp.zeros((KERNEL - 1, pre_conv.shape[1]), jnp.float32), pre_conv.astype(jnp.float32)], 0)
    total = jnp.zeros(pre_conv.shape, jnp.float32)
    for offset in range(KERNEL):
        total = total + taps[offset] * padded[offset:offset + length]
    return jax.nn.silu(total)

def slot_numbers(flat_ids):
    onehot = (flat_ids[:, None] == jnp.arange(EXPERTS, dtype=jnp.int32)[None, :]).astype(jnp.int32)
    before = jnp.cumsum(onehot, axis=0) - onehot
    return lax.optimization_barrier(jnp.sum(before * onehot, axis=1))

def ssd_block(carried, inputs):
    x_blocks, b_blocks, c_blocks, log_decay, step_size = inputs
    cum_decay = jnp.cumsum(log_decay, axis=0)
    per_group = HEADS // GROUPS
    scores = jnp.einsum('igs,jgs->gij', c_blocks, b_blocks, precision=PRECISE)
    scores = jnp.repeat(scores, per_group, axis=0)
    cum_heads = cum_decay.T
    gap_decay = cum_heads[:, :, None] - cum_heads[:, None, :]
    causal = jnp.arange(BLOCK)[:, None] >= jnp.arange(BLOCK)[None, :]
    decay_mask = jnp.exp(jnp.where(causal[None], gap_decay, -jnp.inf))
    weights = scores * decay_mask * step_size.T[:, None, :]
    y_intra = jnp.einsum('hij,jhp->ihp', weights, x_blocks, precision=PRECISE)
    c_heads = jnp.repeat(c_blocks, per_group, axis=1)
    b_heads = jnp.repeat(b_blocks, per_group, axis=1)
    y_inter = jnp.exp(cum_decay)[:, :, None] * jnp.einsum('ihs,hps->ihp', c_heads, carried, precision=PRECISE)
    tail_factor = jnp.exp(cum_decay[-1][None, :] - cum_decay) * step_size
    updated = jnp.exp(cum_decay[-1])[:, None, None] * carried + jnp.einsum('jh,jhp,jhs->hps', tail_factor, x_blocks, b_heads, precision=PRECISE)
    return (updated, y_intra + y_inter)

def reference(tokens, mamba_gain, w_z, w_x, w_bc, w_dt, dt_bias, a_log, conv_x, conv_bc, skip, norm_gain, w_out, moe_gain, expert_ids, router_weights, w_up, w_down):
    stream = tokens.astype(jnp.float32)
    normed = rms_scale(stream, mamba_gain).astype(jnp.bfloat16)
    gate_in = jnp.dot(normed, w_z, preferred_element_type=jnp.float32).astype(jnp.bfloat16)
    x_in = jnp.dot(normed, w_x, preferred_element_type=jnp.float32).astype(jnp.bfloat16)
    bc_in = jnp.dot(normed, w_bc, preferred_element_type=jnp.float32).astype(jnp.bfloat16)
    step_size = jax.nn.softplus(jnp.dot(normed, w_dt, preferred_element_type=jnp.float32) + dt_bias)
    log_decay = -jnp.exp(a_log) * step_size
    x_conv = causal_conv(x_in, conv_x)
    bc_conv = causal_conv(bc_in, conv_bc).reshape(LENGTH, GROUPS, 2, STATE)
    blocks = LENGTH // BLOCK
    x_blocks = x_conv.reshape(blocks, BLOCK, HEADS, HEAD_DIM)
    b_blocks = bc_conv[:, :, 0].reshape(blocks, BLOCK, GROUPS, STATE)
    c_blocks = bc_conv[:, :, 1].reshape(blocks, BLOCK, GROUPS, STATE)
    start_state = jnp.zeros((HEADS, HEAD_DIM, STATE), jnp.float32)
    _, y_total = lax.scan(ssd_block, start_state, (x_blocks, b_blocks, c_blocks, log_decay.reshape(blocks, BLOCK, HEADS), step_size.reshape(blocks, BLOCK, HEADS)))
    x_heads = x_conv.reshape(LENGTH, HEADS, HEAD_DIM)
    y_total = y_total.reshape(LENGTH, HEADS, HEAD_DIM) + skip[:, None] * x_heads
    gated = y_total * jax.nn.silu(gate_in.astype(jnp.float32)).reshape(LENGTH, HEADS, HEAD_DIM)
    gated = gated * lax.rsqrt(lax.optimization_barrier(jnp.mean(gated * gated, axis=-1, keepdims=True)) + EPSILON)
    gated = (gated.reshape(LENGTH, INNER) * norm_gain).astype(jnp.bfloat16)
    share_width = INNER // N_WIDE

    def add_share(total, wide_index):
        gated_part = lax.dynamic_slice_in_dim(gated, wide_index * share_width, share_width, 1)
        weight_part = lax.dynamic_slice_in_dim(w_out, wide_index * share_width, share_width, 0)
        partial_sum = jnp.dot(gated_part, weight_part, preferred_element_type=jnp.float32).astype(jnp.bfloat16)
        partial_sum = lax.optimization_barrier(partial_sum)
        return (total + partial_sum.astype(jnp.float32), None)
    mamba_out, _ = lax.scan(add_share, jnp.zeros((LENGTH, D), jnp.float32), jnp.arange(N_WIDE, dtype=jnp.int32))
    hidden_stream = (stream + mamba_out).astype(jnp.bfloat16)
    hidden_f32 = hidden_stream.astype(jnp.float32)
    moe_in = rms_scale(hidden_f32, moe_gain).astype(jnp.bfloat16)
    devices = N_CTX * N_WIDE
    flat_ids = expert_ids.reshape(devices, TOK_DEV * TOP)
    slots = jax.vmap(slot_numbers)(flat_ids)
    source = jnp.arange(devices, dtype=jnp.int32)[:, None]
    row_index = jnp.arange(TOK_DEV * TOP, dtype=jnp.int32)[None, :]
    token_index = source * TOK_DEV + row_index // TOP
    slot_index = flat_ids * (devices * CAP) + source * CAP + slots
    slot_table = jnp.full((EXPERTS * devices * CAP,), LENGTH, jnp.int32).at[slot_index.reshape(-1)].set(token_index.reshape(-1))
    slot_weight = jnp.zeros((EXPERTS * devices * CAP,), jnp.float32).at[slot_index.reshape(-1)].set(router_weights.reshape(-1))
    padded_in = jnp.concatenate([moe_in, jnp.zeros((1, D), jnp.bfloat16)], 0)

    def run_expert(accumulated, expert_index):
        slot_rows = lax.dynamic_slice_in_dim(slot_table, expert_index * devices * CAP, devices * CAP, 0)
        row_weight = lax.dynamic_slice_in_dim(slot_weight, expert_index * devices * CAP, devices * CAP, 0)
        picked_rows = padded_in[slot_rows]
        up_proj = jnp.dot(picked_rows, w_up[expert_index], preferred_element_type=jnp.float32)
        activated = jax.nn.relu(up_proj)
        activated = (activated * activated).astype(jnp.bfloat16)
        expert_out = jnp.dot(activated, w_down[expert_index], preferred_element_type=jnp.float32).astype(jnp.bfloat16)
        contrib = expert_out.astype(jnp.float32) * row_weight[:, None]
        return (accumulated.at[slot_rows].add(contrib), None)
    accumulated, _ = lax.scan(run_expert, jnp.zeros((LENGTH + 1, D), jnp.float32), jnp.arange(EXPERTS, dtype=jnp.int32))
    return (hidden_f32 + accumulated[:LENGTH]).astype(jnp.bfloat16)
```

```python
import functools

import jax
import jax.numpy as jnp
from jax import lax
from jax.experimental import pallas as pl
from jax.experimental.pallas import tpu as pltpu
from jax.sharding import PartitionSpec as P

STATE = 128
GROUPS = 8
KERNEL = 4
TOP = 6
BLOCK = 128
HEAD_DIM = 64
RIM = 8

EPSILON = 1e-05
PRECISE = lax.Precision.HIGHEST
BF16 = jnp.bfloat16
F32 = jnp.float32


def shifted(block, axis, distance):
    devices = range(lax.axis_size(axis))
    route = [(i - distance, i) for i in devices if i - distance in devices]
    return lax.ppermute(block, axis, route)


def rms_scale(values, gain_vec):
    mean_sq = jnp.mean(values * values, axis=-1, keepdims=True)
    return values * lax.rsqrt(mean_sq + EPSILON) * gain_vec


def by_head(columns, width):
    rows, heads = columns.shape
    lane_head = lax.broadcasted_iota(jnp.int32, (rows, width), 1) // HEAD_DIM
    out = jnp.broadcast_to(columns[:, 0:1], (rows, width))
    for h in range(1, heads):
        out = jnp.where(lane_head == h, columns[:, h : h + 1], out)
    return out


def scan_kernel(
    heads, proj_ref, rim_ref, taps_ref, skip_ref, steps_ref, steps_t_ref,
    y_ref, c_ref, cum_ref, state_ref, ext, running,
):
    n = pl.program_id(0)
    width = heads * HEAD_DIM
    columns = width + 2 * STATE

    @pl.when(n == 0)
    def _():
        ext[0:RIM, :] = rim_ref[...].astype(F32)
        state_ref[...] = jnp.zeros_like(state_ref)
        running[...] = jnp.zeros_like(running)

    @pl.when(n > 0)
    def _():
        ext[0:RIM, :] = ext[BLOCK : BLOCK + RIM, :]

    ext[RIM : RIM + BLOCK, :] = proj_ref[:, width:].astype(F32)
    total = jnp.zeros((BLOCK, columns), F32)
    for tap in range(KERNEL):
        start = RIM - (KERNEL - 1) + tap
        total = total + taps_ref[tap : tap + 1, :] * ext[start : start + BLOCK, :]
    conved = total * jax.nn.sigmoid(total)
    x = conved[:, :width]
    b = conved[:, width : width + STATE].astype(BF16)
    c = conved[:, width + STATE :].astype(BF16)

    row = lax.broadcasted_iota(jnp.int32, (BLOCK, BLOCK), 0)
    col = lax.broadcasted_iota(jnp.int32, (BLOCK, BLOCK), 1)
    causal = row >= col
    lower = causal.astype(F32)
    upper = (row <= col).astype(F32)
    steps = steps_ref[...]
    cum = jnp.dot(lower, steps, precision=PRECISE, preferred_element_type=F32)
    cum_t = jnp.dot(steps_t_ref[...], upper, precision=PRECISE, preferred_element_type=F32)
    decay = cum[:, heads : 2 * heads]
    x_step = x * by_head(steps[:, :heads], width)
    x_bf = x_step.astype(BF16)
    scores = lax.dot_general(c, b, (((1,), (1,)), ((), ())), preferred_element_type=F32)
    lane_head = lax.broadcasted_iota(jnp.int32, (BLOCK, width), 1) // HEAD_DIM
    y = None
    for h in range(heads):
        gap = decay[:, h : h + 1] - cum_t[heads + h : heads + h + 1, :]
        weight = scores * jnp.exp(jnp.where(causal, gap, -jnp.inf))
        part = jnp.dot(weight.astype(BF16), x_bf, preferred_element_type=F32)
        y = part if y is None else jnp.where(lane_head == h, part, y)
    state = state_ref[...]
    y = y + by_head(jnp.exp(decay), width) * jnp.dot(
        c, state.astype(BF16), preferred_element_type=F32
    )
    y_ref[...] = y + skip_ref[...] * x
    c_ref[...] = c
    last = decay[BLOCK - 1 : BLOCK, :]
    tail = (x_step * by_head(jnp.exp(last - decay), width)).astype(BF16)
    state_ref[...] = by_head(jnp.exp(last), width) * state + lax.dot_general(
        b, tail, (((0,), (0,)), ((), ())), preferred_element_type=F32
    )
    span_cum = cum + running[0:1, :]
    cum_ref[...] = span_cum
    running[...] = jnp.broadcast_to(span_cum[BLOCK - 1 : BLOCK, :], running.shape)


def scan_blocks(projected, rim, taps, skip_row, steps, steps_t, heads):
    rows = projected.shape[0]
    width = heads * HEAD_DIM
    blocks = rows // BLOCK
    return pl.pallas_call(
        functools.partial(scan_kernel, heads),
        grid=(blocks,),
        in_specs=[
            pl.BlockSpec((BLOCK, projected.shape[1]), lambda n: (n, 0)),
            pl.BlockSpec(rim.shape, lambda n: (0, 0)),
            pl.BlockSpec(taps.shape, lambda n: (0, 0)),
            pl.BlockSpec(skip_row.shape, lambda n: (0, 0)),
            pl.BlockSpec((BLOCK, 2 * heads), lambda n: (n, 0)),
            pl.BlockSpec((2 * heads, BLOCK), lambda n: (0, n)),
        ],
        out_specs=[
            pl.BlockSpec((BLOCK, width), lambda n: (n, 0)),
            pl.BlockSpec((BLOCK, STATE), lambda n: (n, 0)),
            pl.BlockSpec((BLOCK, 2 * heads), lambda n: (n, 0)),
            pl.BlockSpec((STATE, width), lambda n: (0, 0)),
        ],
        out_shape=[
            jax.ShapeDtypeStruct((rows, width), F32),
            jax.ShapeDtypeStruct((rows, STATE), BF16),
            jax.ShapeDtypeStruct((rows, 2 * heads), F32),
            jax.ShapeDtypeStruct((STATE, width), F32),
        ],
        scratch_shapes=[
            pltpu.VMEM((RIM + BLOCK, width + 2 * STATE), F32),
            pltpu.VMEM((8, 2 * heads), F32),
        ],
        cost_estimate=pl.CostEstimate(
            flops=blocks * 2 * BLOCK * BLOCK * width * 7, bytes_accessed=rows * 4000,
            transcendentals=rows * 1000,
        ),
        name="scan_blocks",
    )(projected, rim, taps, skip_row, steps, steps_t)


def finish_rows(heads, y, c, cum, gate, incoming, gain):
    width = heads * HEAD_DIM
    decay = jnp.exp(cum[:, heads : 2 * heads])
    y = y + by_head(decay, width) * jnp.dot(c, incoming, preferred_element_type=F32)
    gate = gate.astype(F32)
    gated = y * (gate * jax.nn.sigmoid(gate))
    square = gated * gated
    lane_head = lax.broadcasted_iota(jnp.int32, square.shape, 1) // HEAD_DIM
    means = [
        jnp.sum(jnp.where(lane_head == h, square, 0.0), axis=1, keepdims=True) for h in range(heads)
    ]
    mean_sq = by_head(jnp.concatenate(means, axis=1), width) * (1.0 / HEAD_DIM)
    return (gated * lax.rsqrt(mean_sq + EPSILON) * gain).astype(BF16)


def finish_kernel(heads, y_ref, c_ref, cum_ref, gate_ref, incoming_ref, gain_ref, w_ref, out_ref):
    gated = finish_rows(
        heads, y_ref[...], c_ref[...], cum_ref[...], gate_ref[...], incoming_ref[...], gain_ref[...]
    )
    out_ref[...] = jnp.dot(gated, w_ref[...], preferred_element_type=F32).astype(BF16)


def finish_blocks(y, c, cum, projected, incoming, gain_row, w_out, heads):
    rows, width = y.shape
    model_width = w_out.shape[1]
    blocks = rows // BLOCK
    return pl.pallas_call(
        functools.partial(finish_kernel, heads),
        grid=(blocks,),
        in_specs=[
            pl.BlockSpec((BLOCK, width), lambda n: (n, 0)),
            pl.BlockSpec((BLOCK, STATE), lambda n: (n, 0)),
            pl.BlockSpec((BLOCK, 2 * heads), lambda n: (n, 0)),
            pl.BlockSpec((BLOCK, width), lambda n: (n, 0)),
            pl.BlockSpec(incoming.shape, lambda n: (0, 0)),
            pl.BlockSpec(gain_row.shape, lambda n: (0, 0)),
            pl.BlockSpec(w_out.shape, lambda n: (0, 0)),
        ],
        out_specs=pl.BlockSpec((BLOCK, model_width), lambda n: (n, 0)),
        out_shape=jax.ShapeDtypeStruct((rows, model_width), BF16),
        cost_estimate=pl.CostEstimate(
            flops=2 * rows * width * model_width, bytes_accessed=rows * (model_width * 2 + 2000),
            transcendentals=rows * width,
        ),
        name="finish_blocks",
    )(y, c, cum, projected, incoming, gain_row, w_out)


def route_tables(expert_ids, router_weights, experts, slots):
    tok_rows = expert_ids.shape[0]
    named = expert_ids[:, :, None] == jnp.arange(experts, dtype=jnp.int32)[None, None, :]
    member = jnp.sum(named.astype(F32), axis=1)
    weight = jnp.sum(jnp.where(named, router_weights[:, :, None], 0.0), axis=1)
    strictly = jnp.arange(tok_rows)[:, None] > jnp.arange(tok_rows)[None, :]
    before = jnp.dot(strictly.astype(BF16), member.astype(BF16), preferred_element_type=F32)
    place = jnp.where(member > 0, before, -1.0)
    slot = jnp.arange(slots, dtype=F32)
    hit = place[:, :, None] == slot[None, None, :]
    combine = jnp.where(hit, weight[:, :, None], 0.0).reshape(tok_rows, experts * slots)
    hit_t = place.T[:, None, :] == slot[None, :, None]
    dispatch = hit_t.astype(BF16).reshape(experts * slots, tok_rows)
    high = combine.astype(BF16)
    low = (combine - high.astype(F32)).astype(BF16)
    return dispatch, high, low


def shards(
    tokens,
    mamba_gain,
    w_z,
    w_x,
    w_bc,
    w_dt,
    dt_bias,
    a_log,
    conv_x,
    conv_bc,
    skip,
    norm_gain,
    w_out,
    moe_gain,
    expert_ids,
    router_weights,
    w_up,
    w_down,
):
    wide_count = lax.axis_size("wide")
    ctx_count = lax.axis_size("ctx")
    tok_rows, model_width = tokens.shape
    heads = dt_bias.shape[0]
    width = heads * HEAD_DIM
    position = lax.axis_index("wide")
    ctx_position = lax.axis_index("ctx")

    experts = ctx_count * wide_count
    capacity = max(2, (7 * tok_rows * TOP + 6 * experts - 1) // (6 * experts))
    slots = -(-capacity // 8) * 8
    dispatch, combine_high, combine_low = route_tables(expert_ids, router_weights, experts, slots)

    stream = tokens.astype(F32)
    normed = rms_scale(stream, mamba_gain).astype(BF16)
    partner_route = [(i, i ^ 1) for i in range(wide_count)]
    partner_bc = lax.ppermute(w_bc, "wide", partner_route)
    upper_half = position % 2 == 1
    weight = jnp.concatenate(
        [w_z, w_x, jnp.where(upper_half, partner_bc, w_bc), jnp.where(upper_half, w_bc, partner_bc)],
        1,
    )
    raw_steps = jnp.dot(normed, w_dt, preferred_element_type=F32)
    steps_here = lax.all_to_all(raw_steps, "wide", split_axis=1, concat_axis=0, tiled=True)
    step_size = jax.nn.softplus(steps_here + dt_bias)
    steps = jnp.concatenate([step_size, -jnp.exp(a_log) * step_size], 1)
    group_index = position // (wide_count // GROUPS)
    taps_group = lax.dynamic_slice_in_dim(conv_bc, group_index * 2 * STATE, 2 * STATE, 1)
    taps = jnp.concatenate([conv_x, taps_group], 1)

    projected = jnp.dot(
        lax.all_gather(normed, "wide", axis=0, tiled=True), weight, preferred_element_type=F32
    ).astype(BF16)
    rim = shifted(projected[-RIM:, width:], "ctx", 1)
    skip_row = jnp.repeat(skip, HEAD_DIM)[None, :]
    y, c, cum, span_state = scan_blocks(
        projected, rim, taps, skip_row, steps, steps.T, heads
    )

    span_decay = cum[-1, heads:]
    packed = jnp.concatenate(
        [span_state, jnp.broadcast_to(jnp.repeat(span_decay, HEAD_DIM)[None, :], (8, width))], 0
    )
    spans = lax.all_gather(packed, "ctx", axis=0)
    states = spans[:, :STATE]
    decays = spans[:, STATE]
    index = jnp.arange(ctx_count)
    between = (index[None, :] > index[:, None]) & (index[None, :] < ctx_position)
    gap = jnp.sum(jnp.where(between[:, :, None], decays[None, :, :], 0.0), axis=1)
    factor = jnp.where((index < ctx_position)[:, None], jnp.exp(gap), 0.0)
    incoming = jnp.sum(factor[:, None, :] * states, axis=0).astype(BF16)

    partial_out = finish_blocks(
        y, c, cum, projected, incoming, norm_gain[None, :], w_out, heads
    )
    mamba_out = lax.psum_scatter(
        partial_out, "wide", scatter_dimension=0, tiled=True
    ).astype(F32)
    hidden_stream = (stream + mamba_out).astype(BF16)
    hidden_f32 = hidden_stream.astype(F32)
    moe_in = rms_scale(hidden_f32, moe_gain).astype(BF16)

    outgoing = jnp.dot(dispatch, moe_in, preferred_element_type=F32).astype(BF16)
    arrived = lax.all_to_all(
        outgoing.reshape(experts, slots, model_width),
        ("ctx", "wide"), split_axis=0, concat_axis=0, tiled=True,
    ).reshape(experts * slots, model_width)
    up_proj = jnp.dot(arrived, w_up[0], preferred_element_type=F32)
    activated = jax.nn.relu(up_proj)
    activated = (activated * activated).astype(BF16)
    expert_out = jnp.dot(activated, w_down[0], preferred_element_type=F32).astype(BF16)
    returned = lax.all_to_all(
        expert_out.reshape(experts, slots, model_width),
        ("ctx", "wide"), split_axis=0, concat_axis=0, tiled=True,
    ).reshape(experts * slots, model_width)
    combined = jnp.dot(combine_high, returned, preferred_element_type=F32) + jnp.dot(
        combine_low, returned, preferred_element_type=F32
    )
    return (hidden_f32 + combined).astype(BF16)


def solution(mesh):
    placed = (
        P(("ctx", "wide"), None),
        P(),
        P(None, "wide"),
        P(None, "wide"),
        P(None, "wide"),
        P(),
        P("wide"),
        P("wide"),
        P(None, "wide"),
        P(),
        P("wide"),
        P("wide"),
        P("wide", None),
        P(),
        P(("ctx", "wide"), None),
        P(("ctx", "wide"), None),
        P(("ctx", "wide"), None, None),
        P(("ctx", "wide"), None, None),
    )
    return jax.shard_map(
        shards, mesh=mesh, in_specs=placed, out_specs=P(("ctx", "wide"), None), check_vma=False
    )
```
